512 devices in a mesh: depth: 64 (over z_lo, y, core), cols: 8 (over x, z_hi).
Axes of the slice: x: 4, y: 8, z: 8 (z_hi: 2, z_lo: 4; z = z_hi * 4 + z_lo), core: 2. Of those that a mesh axis runs over, the one named last changes fastest.
Arguments:
- field: float32 [128, 2048, 1024], P('depth', None, 'cols'), may hold values from -6 to 6
Outputs:
- picture: float32 [4, 2048, 1024], P(None, 'depth', 'cols')
The draws below stay inside these ranges and needn't reach their ends.
All inputs are finite; a program needn't handle non-finite values.
Results may differ from the reference program's by a relative error of at most 0.00002.
Values sent between devices are 32-bit elements; how exact they have to be, the bound alone decides.
A program may use at most 128 MiB of HBM per device.

```python
import math
import jax
import jax.numpy as jnp
from jax import lax

ROWS = 2048
NZ = 128
WIDTH = 1024


def block_levels(stream_key, dims, cuts, low, high):
    gain, own = 1.0, jax.random.fold_in(stream_key, 6)
    for dim, shards_of in cuts:
        heights = jnp.exp(jax.random.uniform(jax.random.fold_in(own, dim), (shards_of,), jnp.float32, low / len(cuts), high / len(cuts)))
        gain = gain * jnp.repeat(heights, dims[dim] // shards_of).reshape([-1 if axis == dim else 1 for axis in range(len(dims))])
    return gain


def noise(own_key, dims, spread, reach, cuts=(), dtype=jnp.bfloat16):
    entries = spread * jax.random.normal(own_key, dims, jnp.float32)
    if cuts:
        entries = entries * block_levels(own_key, dims, cuts, -0.22, 0.18)
    return jnp.clip(entries, -reach, reach).astype(dtype)


def setup_inputs(seed: int = 0) -> dict:
    key_of = jax.random.split(jax.random.key(seed), 2)
    field = noise(key_of[0], (NZ, ROWS, WIDTH), 1.0, 6.0, ((0, 64), (2, 8)), jnp.float32)
    return {"field": field}


def apply_taps(array_in, tap_list, which_axis):
    length = array_in.shape[which_axis] - 4
    result = tap_list[0] * lax.slice_in_dim(array_in, 0, length, axis=which_axis)
    for offset in range(1, 5):
        result = result + tap_list[offset] * lax.slice_in_dim(array_in, offset, offset + length, axis=which_axis)
    return result

def render_slab(padded):
    gauss_taps = [1.0 / 16, 4.0 / 16, 6.0 / 16, 4.0 / 16, 1.0 / 16]
    deriv_taps = [-1.0 / 8, -2.0 / 8, 0.0, 2.0 / 8, 1.0 / 8]
    smooth_x = apply_taps(padded, gauss_taps, 2)
    deriv_x = apply_taps(padded, deriv_taps, 2)
    smooth_xy = apply_taps(smooth_x, gauss_taps, 1)
    deriv_y = apply_taps(smooth_x, deriv_taps, 1)
    deriv_xy = apply_taps(deriv_x, gauss_taps, 1)
    smooth = apply_taps(smooth_xy, gauss_taps, 0)
    grad_z = 8.0 * apply_taps(smooth_xy, deriv_taps, 0)
    grad_y = 8.0 * apply_taps(deriv_y, gauss_taps, 0)
    grad_x = 8.0 * apply_taps(deriv_xy, gauss_taps, 0)
    scaled = 7.0 * smooth
    opacity = 0.6 * jax.nn.sigmoid(6.0 * scaled - 13.2)
    norm_len = jnp.sqrt(grad_x * grad_x + grad_y * grad_y + grad_z * grad_z + 1.0)
    half_len = math.sqrt(0.48 * 0.48 + 0.6 * 0.6 + 1.64 * 1.64)
    dot_light = (0.48 * grad_x + 0.6 * grad_y + 0.64 * grad_z) / norm_len
    dot_half = (0.48 * grad_x + 0.6 * grad_y + 1.64 * grad_z) / (half_len * norm_len)
    shading = 0.25 + 0.6 * jnp.maximum(dot_light, 0.0) + 0.35 * jnp.maximum(dot_half, 0.0) ** 8
    weight = opacity * shading
    colours = jnp.stack([jax.nn.sigmoid(2.0 * scaled + 0.5) * weight, (0.5 + 0.4 * jnp.tanh(scaled)) * weight, jax.nn.sigmoid(-2.0 * scaled) * weight], 0)
    return (colours, opacity)

def composite_planes(colours, opacity):

    def step_fn(state_pair, plane):
        colour_sum, opacity_sum = state_pair
        plane_colour, plane_opacity = plane
        remain = 1.0 - opacity_sum
        return ((colour_sum + remain[None] * plane_colour, opacity_sum + remain * plane_opacity), None)
    start = (jnp.zeros(colours.shape[0:1] + colours.shape[2:], jnp.float32), jnp.zeros(opacity.shape[1:], jnp.float32))
    final_pair, unused = lax.scan(step_fn, start, (jnp.moveaxis(colours, 1, 0), opacity))
    return jnp.concatenate([final_pair[0], final_pair[1][None]], 0)

def reference(field):
    padded = jnp.pad(field, 2)
    colours, opacity = render_slab(padded)
    return composite_planes(colours, opacity)
```

```python
import functools
import math

import jax
import jax.numpy as jnp
from jax import lax
from jax.experimental import pallas as pl
from jax.experimental.pallas import tpu as pltpu
from jax.sharding import PartitionSpec as P

MESH = pl.DeviceIdType.MESH
F32 = jnp.float32
HALF = math.sqrt(0.48 * 0.48 + 0.6 * 0.6 + 1.64 * 1.64)
ORDER = (0, 1, -1, 2, -2, 3, -3, 4)
NY, NZLO = 8, 4
EARLY = 5


def lanes_of(shape):
    return lax.broadcasted_iota(jnp.int32, shape, 1)


def along_x(x, h):
    lane = lanes_of(x.shape)
    r1 = pltpu.roll(jnp.where(lane == 127, h, x), 1, 1)
    r2 = pltpu.roll(jnp.where(lane >= 126, h, x), 2, 1)
    l1 = pltpu.roll(jnp.where(lane == 0, h, x), 127, 1)
    l2 = pltpu.roll(jnp.where(lane <= 1, h, x), 126, 1)
    gauss = (r2 + l2) + 4.0 * (r1 + l1) + 6.0 * x
    deriv = (l2 - r2) + 2.0 * (l1 - r1)
    return gauss, deriv


def cascade(v):
    for _ in range(3):
        v = [v[k] + v[k + 1] for k in range(len(v) - 1)]
    return v


def shade(s, gz, gy, gx):
    t2 = s * (14.0 / 4096.0)
    e = jnp.exp(-t2)
    sig = 1.0 / (1.0 + e)
    red = 1.0 / (1.0 + math.exp(-0.5) * e)
    op = 0.6 / (1.0 + jnp.exp(jnp.minimum(13.2 - 3.0 * t2, 87.0)))
    inv = lax.rsqrt(gx * gx + gy * gy + (gz * gz + 65536.0))
    dl = 0.48 * gx + 0.6 * gy + 0.64 * gz
    diff = jnp.maximum(dl * inv, 0.0)
    spec = jnp.maximum((dl + gz) * (inv * (1.0 / HALF)), 0.0)
    spec = spec * spec
    spec = spec * spec
    spec = spec * spec
    w = op * (0.25 + 0.6 * diff + 0.35 * spec)
    return op, w, red, 0.1 + 0.8 * sig, e * sig


def kernel(n_depth, n_cols, field, out, fv, wown, wleft, wright, tt, em, rm, re, ht, ug, ud, sf, pim,
           local_sem, wsend, wrecv, msend, mrecv, esend, erecv):
    me = lax.axis_index("depth")
    col = lax.axis_index("cols")
    z, y = me // (2 * NY), me // 2 % NY
    left, right = (col + n_cols - 1) % n_cols, (col + 1) % n_cols
    rows = 2048 // n_depth

    load = pltpu.make_async_copy(field, fv.at[:, pl.ds(8, 2048)], local_sem.at[0])
    load.start()

    barrier = pltpu.get_barrier_semaphore()

    def greet(i, _):
        pl.semaphore_signal(barrier, inc=1, device_id={"depth": (me + i) % n_depth}, device_id_type=MESH)
        return 0

    lax.fori_loop(1, n_depth, greet, 0)
    for other in (left, right):
        pl.semaphore_signal(barrier, inc=1, device_id={"cols": other}, device_id_type=MESH)
    pl.semaphore_wait(barrier, n_depth + 1)

    def peer(o, i):
        return ((z + i // 2) % NZLO) * (2 * NY) + ((y + o + NY) % NY) * 2 + (me + i) % 2

    def main_copy(other, slot):
        return pltpu.make_async_remote_copy(
            src_ref=field.at[:, pl.ds(pl.multiple_of(other * rows, 8), rows)], dst_ref=rm.at[slot],
            send_sem=msend.at[other], recv_sem=mrecv.at[slot],
            device_id={"depth": other}, device_id_type=MESH)

    def edge_copy(other, slot):
        return pltpu.make_async_remote_copy(
            src_ref=em.at[other], dst_ref=re.at[slot],
            send_sem=esend.at[other], recv_sem=erecv.at[slot],
            device_id={"depth": other}, device_id_type=MESH)

    own_main = pltpu.make_async_copy(field.at[:, pl.ds(pl.multiple_of(me * rows, 8), rows)], rm.at[me], local_sem.at[1])
    own_edge = pltpu.make_async_copy(em.at[me], re.at[me], local_sem.at[2])
    own_main.start()

    def each(o, fn):
        lax.fori_loop(1 if o == 0 else 0, 2 * NZLO, lambda i, _: (fn(peer(o, i)), 0)[1], 0)

    for o in ORDER[:EARLY]:
        each(o, lambda other: main_copy(other, me).start())

    load.wait()
    zero = jnp.zeros((8, 128), F32)
    for p in range(2):
        fv[p, 0:8] = zero
        fv[p, 2056:2064] = zero

    def pack(b, _):
        x0 = fv[0, pl.ds(pl.multiple_of(8 + b * 128, 8), 128)]
        x1 = fv[1, pl.ds(pl.multiple_of(8 + b * 128, 8), 128)]
        both = jnp.where(lanes_of(x0.shape) < 4, pltpu.roll(x0, 2, 1), pltpu.roll(x1, 6, 1))
        wown[b] = both.T[0:8]
        return 0

    lax.fori_loop(0, 16, pack, 0)

    to_right = pltpu.make_async_remote_copy(
        src_ref=wown, dst_ref=wleft, send_sem=wsend.at[0], recv_sem=wrecv.at[0],
        device_id={"cols": right}, device_id_type=MESH)
    to_left = pltpu.make_async_remote_copy(
        src_ref=wown, dst_ref=wright, send_sem=wsend.at[1], recv_sem=wrecv.at[1],
        device_id={"cols": left}, device_id_type=MESH)
    to_right.start()
    to_left.start()

    def row_edges(k, _):
        for p in range(2):
            em[k, 4 * p:4 * p + 2] = fv[p, pl.ds(8 + k * rows + rows, 2)]
            em[k, 4 * p + 2:4 * p + 4] = fv[p, pl.ds(8 + k * rows - 2, 2)]
        return 0

    lax.fori_loop(0, n_depth, row_edges, 0)
    tt[0] = zero
    tt[17] = zero
    sub = lax.broadcasted_iota(jnp.int32, (8, 128), 0)
    lane = lanes_of((8, 128))
    from_left = jnp.logical_and(sub % 4 < 2, col > 0)
    from_right = jnp.logical_and(sub % 4 >= 2, col < n_cols - 1)
    to_right.wait()
    to_left.wait()

    def join(b, _):
        tt[b + 1] = jnp.where(from_left, wleft[b], jnp.where(from_right, wright[b], 0.0))
        return 0

    lax.fori_loop(0, 16, join, 0)

    def col_edges(b, _):
        before, here, after = tt[b], tt[b + 1], tt[b + 2]
        for q in range(4):
            turn = (128 - 32 * q) % 128
            main = pltpu.roll(here, turn, 1) if turn else here
            below = pltpu.roll(after, turn, 1) if q == 3 else main
            above = pltpu.roll(before if q == 0 else here, (36 - 32 * q) % 128, 1)
            c = jnp.where(lane < 32, main, jnp.where(lane < 34, below, above))
            c = jnp.where(lane < 36, c, pltpu.roll(c, 4, 1))
            em[4 * b + q, 8:16] = c
        return 0

    lax.fori_loop(0, 16, col_edges, 0)
    own_edge.start()
    for o in ORDER:
        each(o, lambda other: edge_copy(other, me).start())
    for o in ORDER[EARLY:]:
        each(o, lambda other: main_copy(other, me).start())

    for f in range(3):
        for k in (0, 1, 130, 131):
            sf[f, k] = jnp.zeros((32, 128), F32)

    own_edge.wait()
    for o in ORDER:
        each(o, lambda other: edge_copy(other, other).wait_recv())

    def turn_edges(g, _):
        tile = re[pl.ds(g * 16, 16), 8:16].reshape(128, 128)
        ht[g] = tile.T[0:40]
        return 0

    lax.fori_loop(0, NZLO, turn_edges, 0)

    def filter_xy(src):
        group, base = src // 16, src % 16 * 8
        for p in range(2):
            h = pltpu.roll(ht[group, 0:32], (254 - base - 4 * p) % 128, 1)
            g, d = along_x(rm[src, p], h)
            ug[p, 8:40] = g
            ud[p, 8:40] = d
        h = ht[group, 32:40]
        h = jnp.where(sub < 4, pltpu.roll(h, (254 - base) % 128, 1), pltpu.roll(h, (250 - base) % 128, 1))
        g, d = along_x(re[src, 0:8], h)
        for p in range(2):
            ug[p, 40:42] = g[4 * p:4 * p + 2]
            ug[p, 6:8] = g[4 * p + 2:4 * p + 4]
            ud[p, 40:42] = d[4 * p:4 * p + 2]
            ud[p, 6:8] = d[4 * p + 2:4 * p + 4]
        for p in range(2):
            plane = 2 + 2 * src + p
            a, b, c, d, e = (ug[p, 6 + k:38 + k] for k in range(5))
            sf[0, plane] = (a + e) + 4.0 * (b + d) + 6.0 * c
            sf[1, plane] = (e - a) + 2.0 * (d - b)
            a, b, c, d, e = (ud[p, 6 + k:38 + k] for k in range(5))
            sf[2, plane] = (a + e) + 4.0 * (b + d) + 6.0 * c

    def render(grp):
        for j in range(4):
            s, ty, tx = ([sf[f, 4 * grp + k, 8 * j:8 * j + 8] for k in range(8)] for f in range(3))
            s, ty, tx = cascade(s), cascade(ty), cascade(tx)
            for m in range(4):
                op, w, red, green, blue = shade(s[m] + s[m + 1], s[m + 1] - s[m], ty[m] + ty[m + 1], tx[m] + tx[m + 1])
                if m == 0:
                    cr, cg, cb, ca = w * red, w * green, w * blue, op
                else:
                    rest = 1.0 - ca
                    w = rest * w
                    cr, cg, cb, ca = cr + w * red, cg + w * green, cb + w * blue, ca + rest * op
            for i, v in enumerate((cr, cg, cb, ca)):
                pim[grp, i, 8 * j:8 * j + 8] = v

    own_main.wait()

    def arrived(src):
        main_copy(src, src).wait_recv()

    def step(o):
        each(o, arrived)
        lax.fori_loop(0, 2 * NZLO, lambda i, _: (filter_xy(peer(o, i)), 0)[1], 0)

    def show(o):
        lax.fori_loop(0, NZLO, lambda i, _: (render(i * NY + (y + o + NY) % NY), 0)[1], 0)

    step(0)
    for k in (1, 2, 3):
        step(k)
        step(-k)
        if k == 1:
            show(0)
        else:
            show(k - 1)
            show(1 - k)
    step(4)
    show(3)
    show(-3)
    show(4)

    for j in range(4):
        at = pl.ds(8 * j, 8)

        def over(k, acc):
            cr, cg, cb, ca = acc
            rest = 1.0 - ca
            return (cr + rest * pim[k, 0, at], cg + rest * pim[k, 1, at], cb + rest * pim[k, 2, at], ca + rest * pim[k, 3, at])

        for i, v in enumerate(lax.fori_loop(0, n_depth // 2, over, (zero, zero, zero, zero))):
            out[i, at] = v

    to = [main_copy, edge_copy]
    for copy in to:
        for o in ORDER:
            each(o, lambda other: copy(other, me).wait_send())


def solution(mesh):
    n_depth, n_cols = mesh.shape["depth"], mesh.shape["cols"]

    def local(field):
        planes, total, width = field.shape
        rows = total // n_depth
        vmem = lambda *shape: pltpu.VMEM(shape, F32)
        dma = lambda n: pltpu.SemaphoreType.DMA((n,))
        return pl.pallas_call(
            functools.partial(kernel, n_depth, n_cols),
            out_shape=jax.ShapeDtypeStruct((4, rows, width), F32),
            in_specs=[pl.BlockSpec(memory_space=pl.ANY)],
            out_specs=pl.BlockSpec(memory_space=pltpu.VMEM),
            scratch_shapes=[
                vmem(2, total + 16, width),
                vmem(16, 8, 128), vmem(16, 8, 128), vmem(16, 8, 128), vmem(18, 8, 128),
                vmem(n_depth, 16, 128),
                vmem(n_depth, 2, rows, width), vmem(n_depth, 16, 128),
                vmem(4, 40, 128),
                vmem(2, 48, 128), vmem(2, 48, 128),
                vmem(3, 132, rows, width),
                vmem(n_depth // 2, 4, rows, width),
                dma(3), dma(2), dma(2), dma(n_depth), dma(n_depth), dma(n_depth), dma(n_depth),
            ],
            compiler_params=pltpu.CompilerParams(collective_id=0, has_side_effects=True, vmem_limit_bytes=48 << 20),
        )(field)

    return jax.shard_map(local, mesh=mesh, in_specs=(P("depth", None, "cols"),), out_specs=P(None, "depth", "cols"), check_vma=False)
```

```python
import functools
import math

import jax
import jax.numpy as jnp
from jax import lax
from jax.experimental import pallas as pl
from jax.experimental.pallas import tpu as pltpu
from jax.sharding import PartitionSpec as P

MESH = pl.DeviceIdType.MESH
F32 = jnp.float32
HALF = math.sqrt(0.48 * 0.48 + 0.6 * 0.6 + 1.64 * 1.64)
ORDER = (0, 1, -1, 2, -2, 3, -3, 4)
NY, NZLO = 8, 4
TURNS = (2, 3, 1, 0)
SENT = [(o, k) for d in (1, 2, 3) for k in TURNS for o in (d, -d)] + [(4, k) for k in TURNS]
EARLY = 16


def lanes_of(shape):
    return lax.broadcasted_iota(jnp.int32, shape, 1)


def along_x(x, h):
    lane = lanes_of(x.shape)
    r1 = pltpu.roll(jnp.where(lane == 127, h, x), 1, 1)
    r2 = pltpu.roll(jnp.where(lane >= 126, h, x), 2, 1)
    l1 = pltpu.roll(jnp.where(lane == 0, h, x), 127, 1)
    l2 = pltpu.roll(jnp.where(lane <= 1, h, x), 126, 1)
    gauss = (r2 + l2) + 4.0 * (r1 + l1) + 6.0 * x
    deriv = (l2 - r2) + 2.0 * (l1 - r1)
    return gauss, deriv


def cascade(v):
    for _ in range(3):
        v = [v[k] + v[k + 1] for k in range(len(v) - 1)]
    return v


def shade(s, gz, gy, gx):
    t2 = s * (14.0 / 4096.0)
    e = jnp.exp(-t2)
    sig = 1.0 / (1.0 + e)
    red = 1.0 / (1.0 + math.exp(-0.5) * e)
    op = 0.6 / (1.0 + jnp.exp(jnp.minimum(13.2 - 3.0 * t2, 87.0)))
    inv = lax.rsqrt(gx * gx + gy * gy + (gz * gz + 65536.0))
    dl = 0.48 * gx + 0.6 * gy + 0.64 * gz
    diff = jnp.maximum(dl * inv, 0.0)
    spec = jnp.maximum((dl + gz) * (inv * (1.0 / HALF)), 0.0)
    spec = spec * spec
    spec = spec * spec
    spec = spec * spec
    w = op * (0.25 + 0.6 * diff + 0.35 * spec)
    return op, w, red, 0.1 + 0.8 * sig, e * sig


def kernel(n_depth, n_cols, field, out, fv, wlast, wfirst, wleft, wright, tt, em, e1, e2, e3, a1, a2, a3, ht, ug, ud, sf, pim,
           local_sem, wsend, wrecv, s1, m1, s2, m2, s3, m3, es1, er1, es2, er2, es3, er3):
    me = lax.axis_index("depth")
    col = lax.axis_index("cols")
    z, y, core = me // (2 * NY), me // 2 % NY, me % 2
    left, right = (col + n_cols - 1) % n_cols, (col + 1) % n_cols
    block, span = 64, NY * 64

    load = pltpu.make_async_copy(field, fv.at[:, pl.ds(8, NZLO * span)], local_sem.at[0])
    load.start()

    def depth_of(zz, yy, cc):
        return {"depth": zz * (2 * NY) + yy * 2 + cc}

    def copy(src, dst, send, recv, where):
        return pltpu.make_async_remote_copy(
            src_ref=src, dst_ref=dst, send_sem=send, recv_sem=recv, device_id=where, device_id_type=MESH)

    def at_y(o):
        return (y + o + NY) % NY

    def at_z(k):
        return (z + k + NZLO) % NZLO

    partner = depth_of(z, y, 1 - core)
    barrier = pltpu.get_barrier_semaphore()

    def greet(where):
        pl.semaphore_signal(barrier, inc=1, device_id=where, device_id_type=MESH)

    for o in ORDER[1:]:
        greet(depth_of(z, at_y(o), core))
    for k in range(1, NZLO):
        greet(depth_of(at_z(k), y, core))
    greet(partner)
    greet({"cols": left})
    greet({"cols": right})
    pl.semaphore_wait(barrier, NY - 1 + NZLO - 1 + 3)

    def rows_of(zz, yy):
        return fv.at[:, pl.ds(pl.multiple_of(8 + zz * span + yy * block, 8), block)]

    def hop1(o, k):
        yy = at_y(o)
        dst = a2.at[z, y] if k == 0 else a1.at[y, k - 1]
        return copy(rows_of(at_z(k), yy), dst, s1.at[yy * NZLO + k], m1.at[y * NZLO + k], depth_of(z, yy, core))

    def got1(o, k):
        yy = at_y(o)
        dst = a2.at[z, yy] if k == 0 else a1.at[yy, k - 1]
        return copy(rows_of(at_z(k), yy), dst, s1.at[yy * NZLO + k], m1.at[yy * NZLO + k], depth_of(z, yy, core))

    def hop2(o, k):
        yy, zz = at_y(o), at_z(k)
        src = rows_of(zz, yy) if o == 0 else a1.at[yy, k - 1]
        return copy(src, a2.at[z, yy], s2.at[yy * NZLO + k], m2.at[z * NY + yy], depth_of(zz, y, core))

    def got2(o, k):
        yy, zz = at_y(o), at_z(-k)
        return copy(a2.at[zz, yy], a2.at[zz, yy], s2.at[yy * NZLO + k], m2.at[zz * NY + yy], depth_of(zz, y, core))

    def hop3(o, k):
        yy, zz = at_y(o), at_z(-k)
        src = a2.at[zz, yy, :, pl.ds(pl.multiple_of(24 * (1 - core), 8), 40)]
        return copy(src, a3.at[zz, yy], s3.at[zz * NY + yy], m3.at[zz * NY + yy], partner)

    load.wait()
    own = pltpu.make_async_copy(rows_of(z, y), a2.at[z, y], local_sem.at[1])
    own.start()
    for o, k in SENT[:EARLY]:
        hop1(o, k).start()
    for k in TURNS[:-1]:
        hop2(0, k).start()
    zero = jnp.zeros((8, 128), F32)
    for p in range(2):
        fv[p, 0:8] = zero
        fv[p, 2056:2064] = zero
    own.wait()
    hop3(0, 0).start()

    def edges_of(b):
        x0 = fv[0, pl.ds(pl.multiple_of(8 + b * 128, 8), 128)]
        x1 = fv[1, pl.ds(pl.multiple_of(8 + b * 128, 8), 128)]
        both = jnp.where(lanes_of(x0.shape) < 4, pltpu.roll(x0, 2, 1), pltpu.roll(x1, 6, 1))
        return both.T[0:8]

    sub = lax.broadcasted_iota(jnp.int32, (8, 128), 0)
    lane = lanes_of((8, 128))
    is_last = sub % 4 < 2

    def pack(b, _):
        even, odd = edges_of(2 * b), edges_of(2 * b + 1)
        wlast[b] = jnp.where(is_last, even, pltpu.roll(odd, 2, 0))
        wfirst[b] = jnp.where(is_last, pltpu.roll(odd, 6, 0), even)
        return 0

    lax.fori_loop(0, 8, pack, 0)
    to_right = copy(wlast, wleft, wsend.at[0], wrecv.at[0], {"cols": right})
    to_left = copy(wfirst, wright, wsend.at[1], wrecv.at[1], {"cols": left})
    to_right.start()
    to_left.start()

    def row_edges(k, _):
        yy, zz = k // NZLO, k % NZLO
        first = 8 + zz * span + yy * block
        for p in range(2):
            em[yy, zz, 4 * p:4 * p + 2] = fv[p, pl.ds(first + block, 2)]
            em[yy, zz, 4 * p + 2:4 * p + 4] = fv[p, pl.ds(first - 2, 2)]
        return 0

    lax.fori_loop(0, NY * NZLO, row_edges, 0)
    for f in range(3):
        for k in (0, 1, 130, 131):
            sf[f, k] = jnp.zeros((32, 128), F32)
    tt[0] = zero
    tt[17] = zero
    to_right.wait()
    to_left.wait()

    def join(b, _):
        wl = jnp.where(col > 0, wleft[b], 0.0)
        wr = jnp.where(col < n_cols - 1, wright[b], 0.0)
        tt[2 * b + 1] = jnp.where(is_last, wl, wr)
        tt[2 * b + 2] = jnp.where(is_last, pltpu.roll(wl, 6, 0), pltpu.roll(wr, 2, 0))
        return 0

    lax.fori_loop(0, 8, join, 0)

    def col_edges(b, _):
        before, here, after = tt[b], tt[b + 1], tt[b + 2]
        for q in range(2):
            main = pltpu.roll(here, 64, 1) if q else here
            below = pltpu.roll(after, 64, 1) if q else here
            above = pltpu.roll(here if q else before, 4 + 64 * (1 - q), 1)
            c = jnp.where(lane < 64, main, jnp.where(lane < 66, below, above))
            c = jnp.where(lane < 68, c, pltpu.roll(c, 4, 1))
            k = 2 * b + q
            em[k % NY, k // NY, 8:16] = c
        return 0

    lax.fori_loop(0, 16, col_edges, 0)

    def edge1(o, mine):
        yy = at_y(o)
        slot = y if mine else yy
        return copy(em.at[yy], e1.at[slot], es1.at[yy], er1.at[slot], depth_of(z, yy, core))

    def edge2(k, mine):
        zz = at_z(k) if mine else at_z(-k)
        slot = z if mine else zz
        return copy(e1.at[:, zz], e2.at[slot], es2.at[k], er2.at[slot], depth_of(zz, y, core))

    edge3 = copy(e2, e3, es3.at[0], er3.at[0], partner)

    for o in ORDER[1:]:
        edge1(o, True).start()
    for o, k in SENT[EARLY:]:
        hop1(o, k).start()
    e1[y] = em[y]

    def filter_xy(zz, yy, tile, edges, src_core, base):
        h = ht[zz, 64:72]
        h = jnp.where(sub < 4, pltpu.roll(h, (254 - base) % 128, 1), pltpu.roll(h, (250 - base) % 128, 1))
        g, d = along_x(edges[zz, yy, 0:8], h)
        for p in range(2):
            ug[p, 40:42] = g[4 * p:4 * p + 2]
            ug[p, 6:8] = g[4 * p + 2:4 * p + 4]
            ud[p, 40:42] = d[4 * p:4 * p + 2]
            ud[p, 6:8] = d[4 * p + 2:4 * p + 4]
        at = pl.ds(pl.multiple_of(8 - 8 * core, 8), 40)
        for p in range(2):
            h = pltpu.roll(ht[zz, pl.ds(pl.multiple_of(24 * core, 8), 40)], (254 - base - 4 * p) % 128, 1)
            g, d = along_x(tile(zz, yy, p), h)
            ug[p, at] = g
            ud[p, at] = d
        for p in range(2):
            plane = 2 + 2 * (2 * (NY * zz + yy) + src_core) + p
            a, b, c, d, e = (ug[p, 6 + k:38 + k] for k in range(5))
            sf[0, plane] = (a + e) + 4.0 * (b + d) + 6.0 * c
            sf[1, plane] = (e - a) + 2.0 * (d - b)
            a, b, c, d, e = (ud[p, 6 + k:38 + k] for k in range(5))
            sf[2, plane] = (a + e) + 4.0 * (b + d) + 6.0 * c

    def own_tile(zz, yy, p):
        return a2[zz, yy, p, pl.ds(pl.multiple_of(24 * core, 8), 40)]

    def other_tile(zz, yy, p):
        return a3[zz, yy, p]

    def render(grp):
        for j in range(4):
            s, ty, tx = ([sf[f, 4 * grp + k, 8 * j:8 * j + 8] for k in range(8)] for f in range(3))
            s, ty, tx = cascade(s), cascade(ty), cascade(tx)
            for m in range(4):
                op, w, red, green, blue = shade(s[m] + s[m + 1], s[m + 1] - s[m], ty[m] + ty[m + 1], tx[m] + tx[m + 1])
                if m == 0:
                    cr, cg, cb, ca = w * red, w * green, w * blue, op
                else:
                    rest = 1.0 - ca
                    w = rest * w
                    cr, cg, cb, ca = cr + w * red, cg + w * green, cb + w * blue, ca + rest * op
            for i, v in enumerate((cr, cg, cb, ca)):
                pim[grp, i, 8 * j:8 * j + 8] = v

    def pass_on(o, k):
        got1(o, k).wait_recv()
        (hop2 if k else hop3)(o, k).start()

    def pass_over(o, k):
        got2(o, k).wait_recv()
        hop3(o, k).start()

    def forward(o):
        for k in TURNS:
            pass_on(o, k)

    def share(o):
        for k in TURNS[:-1]:
            pass_over(o, k)

    def filter_chip(zz, yy):
        filter_xy(zz, yy, own_tile, e2, core, 8 * yy)
        filter_xy(zz, yy, other_tile, e3, 1 - core, 64 + 8 * yy)

    def step(o, low=0, high=NZLO):
        for i in range(low, high):
            hop3(o, -i).wait_recv()
        lax.fori_loop(low, high, lambda i, _: (filter_chip(at_z(i), at_y(o)), 0)[1], 0)

    def show(o, low=0, high=NZLO):
        lax.fori_loop(low, high, lambda i, _: (render((z + i) % NZLO * NY + at_y(o)), 0)[1], 0)

    forward(1)
    share(0)
    forward(-1)
    share(1)
    forward(2)
    share(-1)
    forward(-2)
    share(2)
    for o in ORDER[1:]:
        edge1(o, False).wait_recv()
    for k in range(1, NZLO):
        edge2(k, True).start()
    for i in range(NY):
        e2[z, i] = e1[i, z]
    share(-2)
    for k in range(1, NZLO):
        edge2(k, False).wait_recv()
    edge3.start()
    edge3.wait_recv()

    def turn_edges(g, _):
        tile = jnp.concatenate([e2[g, :, 8:16].reshape(64, 128), e3[g, :, 8:16].reshape(64, 128)], 0)
        ht[g] = tile.T[0:72]
        return 0

    lax.fori_loop(0, NZLO, turn_edges, 0)

    def both_ways(act, k):
        act(3, k)
        act(-3, k)

    step(0)
    both_ways(pass_on, 2)
    step(1)
    both_ways(pass_on, 3)
    step(-1)
    both_ways(pass_over, 2)
    show(0)
    both_ways(pass_on, 1)
    both_ways(pass_over, 3)
    step(2)
    step(-2)
    both_ways(pass_on, 0)
    both_ways(pass_over, 1)
    show(1)
    show(-1)
    for o in ORDER[1:5]:
        edge1(o, True).wait_send()
        for k in TURNS:
            hop1(o, k).wait_send()
    for o in ORDER[:5]:
        for k in TURNS[:-1]:
            hop2(o, k).wait_send()
        for k in TURNS:
            hop3(o, k).wait_send()
    for k in range(1, NZLO):
        edge2(k, True).wait_send()
    edge3.wait_send()

    def finish(k):
        hop3(4, k).wait_recv()
        zz, yy = at_z(-k), at_y(4)
        filter_chip(zz, yy)
        groups = NY * NZLO
        lax.fori_loop(0, 3, lambda i, _: (render((zz * NY + yy + i - 1 + groups) % groups), 0)[1], 0)

    step(3)
    pass_on(4, 2)
    show(2)
    pass_on(4, 3)
    step(-3)
    pass_over(4, 2)
    pass_on(4, 1)
    show(-2)
    pass_over(4, 3)
    pass_on(4, 0)
    finish(2)
    pass_over(4, 1)
    finish(3)
    finish(0)
    finish(1)

    def over(k, acc):
        cr, cg, cb, ca = acc
        rest = 1.0 - ca
        return (cr + rest * pim[k, 0], cg + rest * pim[k, 1], cb + rest * pim[k, 2], ca + rest * pim[k, 3])

    blank = jnp.zeros((32, 128), F32)
    for i, v in enumerate(lax.fori_loop(0, n_depth // 2, over, (blank, blank, blank, blank))):
        out[i] = v

    for o in ORDER[5:]:
        edge1(o, True).wait_send()
        for k in TURNS:
            hop1(o, k).wait_send()
        for k in TURNS[:-1]:
            hop2(o, k).wait_send()
        for k in TURNS:
            hop3(o, k).wait_send()


def solution(mesh):
    n_depth, n_cols = mesh.shape["depth"], mesh.shape["cols"]

    def local(field):
        planes, total, width = field.shape
        rows = total // n_depth
        vmem = lambda *shape: pltpu.VMEM(shape, F32)
        dma = lambda n: pltpu.SemaphoreType.DMA((n,))
        return pl.pallas_call(
            functools.partial(kernel, n_depth, n_cols),
            out_shape=jax.ShapeDtypeStruct((4, rows, width), F32),
            in_specs=[pl.BlockSpec(memory_space=pltpu.HBM)],
            out_specs=pl.BlockSpec(memory_space=pltpu.VMEM),
            scratch_shapes=[
                vmem(2, total + 16, width),
                vmem(8, 8, 128), vmem(8, 8, 128), vmem(8, 8, 128), vmem(8, 8, 128), vmem(18, 8, 128),
                vmem(NY, NZLO, 16, 128), vmem(NY, NZLO, 16, 128), vmem(NZLO, NY, 16, 128), vmem(NZLO, NY, 16, 128),
                vmem(NY, NZLO - 1, 2, 64, 128), vmem(NZLO, NY, 2, 64, 128), vmem(NZLO, NY, 2, 40, 128),
                vmem(NZLO, 72, 128),
                vmem(2, 48, 128), vmem(2, 48, 128),
                vmem(3, 132, rows, width),
                vmem(n_depth // 2, 4, rows, width),
                dma(2), dma(2), dma(2),
                dma(32), dma(32), dma(32), dma(32), dma(32), dma(32),
                dma(NY), dma(NY), dma(NZLO), dma(NZLO), dma(1), dma(1),
            ],
            compiler_params=pltpu.CompilerParams(collective_id=0, has_side_effects=True, vmem_limit_bytes=63 << 20),
        )(field)

    return jax.shard_map(local, mesh=mesh, in_specs=(P("depth", None, "cols"),), out_specs=P(None, "depth", "cols"), check_vma=False)
```

```python
import functools
import math

import jax
import jax.numpy as jnp
from jax import lax
from jax.experimental import pallas as pl
from jax.experimental.pallas import tpu as pltpu
from jax.sharding import PartitionSpec as P

MESH = pl.DeviceIdType.MESH
F32 = jnp.float32
HALF = math.sqrt(0.48 * 0.48 + 0.6 * 0.6 + 1.64 * 1.64)
ORDER = (0, 1, -1, 2, -2, 3, -3, 4)
NY, NZLO = 8, 4
TURNS = (2, 3, 1, 0)
SENT = [(o, k) for d in (1, 2, 3) for k in TURNS for o in (d, -d)] + [(4, k) for k in TURNS]
EARLY = 12


def lanes_of(shape):
    return lax.broadcasted_iota(jnp.int32, shape, 1)


def along_x(x, h):
    lane = lanes_of(x.shape)
    r1 = pltpu.roll(jnp.where(lane == 127, h, x), 1, 1)
    r2 = pltpu.roll(jnp.where(lane >= 126, h, x), 2, 1)
    l1 = pltpu.roll(jnp.where(lane == 0, h, x), 127, 1)
    l2 = pltpu.roll(jnp.where(lane <= 1, h, x), 126, 1)
    gauss = (r2 + l2) + 4.0 * (r1 + l1) + 6.0 * x
    deriv = (l2 - r2) + 2.0 * (l1 - r1)
    return gauss, deriv


def cascade(v):
    for _ in range(3):
        v = [v[k] + v[k + 1] for k in range(len(v) - 1)]
    return v


def shade(s, gz, gy, gx):
    t2 = s * (14.0 / 4096.0)
    e = jnp.exp(-t2)
    sig = 1.0 / (1.0 + e)
    red = 1.0 / (1.0 + math.exp(-0.5) * e)
    op = 0.6 / (1.0 + jnp.exp(jnp.minimum(13.2 - 3.0 * t2, 87.0)))
    inv = lax.rsqrt(gx * gx + gy * gy + (gz * gz + 65536.0))
    dl = 0.48 * gx + 0.6 * gy + 0.64 * gz
    diff = jnp.maximum(dl * inv, 0.0)
    spec = jnp.maximum((dl + gz) * (inv * (1.0 / HALF)), 0.0)
    spec = spec * spec
    spec = spec * spec
    spec = spec * spec
    w = op * (0.25 + 0.6 * diff + 0.35 * spec)
    return op, w, red, 0.1 + 0.8 * sig, e * sig


def kernel(n_depth, n_cols, field, out, fv, wlast, wfirst, wleft, wright, tt, em, e1, e2, e3, a1, a2, a3, ht, ug, ud, sf, pim,
           local_sem, wsend, wrecv, s1, m1, s2, m2, s3, m3, es1, er1, es2, er2, es3, er3):
    me = lax.axis_index("depth")
    col = lax.axis_index("cols")
    z, y, core = me // (2 * NY), me // 2 % NY, me % 2
    left, right = (col + n_cols - 1) % n_cols, (col + 1) % n_cols
    block, span = 64, NY * 64

    load = pltpu.make_async_copy(field, fv.at[:, pl.ds(8, NZLO * span)], local_sem.at[0])
    load.start()

    def depth_of(zz, yy, cc):
        return {"depth": zz * (2 * NY) + yy * 2 + cc}

    def copy(src, dst, send, recv, where):
        return pltpu.make_async_remote_copy(
            src_ref=src, dst_ref=dst, send_sem=send, recv_sem=recv, device_id=where, device_id_type=MESH)

    def at_y(o):
        return (y + o + NY) % NY

    def at_z(k):
        return (z + k + NZLO) % NZLO

    partner = depth_of(z, y, 1 - core)
    barrier = pltpu.get_barrier_semaphore()

    def greet(where):
        pl.semaphore_signal(barrier, inc=1, device_id=where, device_id_type=MESH)

    for o in ORDER[1:]:
        greet(depth_of(z, at_y(o), core))
    for k in range(1, NZLO):
        greet(depth_of(at_z(k), y, core))
    greet(partner)
    greet({"cols": left})
    greet({"cols": right})
    pl.semaphore_wait(barrier, NY - 1 + NZLO - 1 + 3)

    def rows_of(zz, yy):
        return fv.at[:, pl.ds(pl.multiple_of(8 + zz * span + yy * block, 8), block)]

    def hop1(o, k):
        yy = at_y(o)
        dst = a2.at[z, y] if k == 0 else a1.at[y, k - 1]
        return copy(rows_of(at_z(k), yy), dst, s1.at[yy * NZLO + k], m1.at[y * NZLO + k], depth_of(z, yy, core))

    def got1(o, k):
        yy = at_y(o)
        dst = a2.at[z, yy] if k == 0 else a1.at[yy, k - 1]
        return copy(rows_of(at_z(k), yy), dst, s1.at[yy * NZLO + k], m1.at[yy * NZLO + k], depth_of(z, yy, core))

    def hop2(o, k):
        yy, zz = at_y(o), at_z(k)
        src = rows_of(zz, yy) if o == 0 else a1.at[yy, k - 1]
        return copy(src, a2.at[z, yy], s2.at[yy * NZLO + k], m2.at[z * NY + yy], depth_of(zz, y, core))

    def got2(o, k):
        yy, zz = at_y(o), at_z(-k)
        return copy(a2.at[zz, yy], a2.at[zz, yy], s2.at[yy * NZLO + k], m2.at[zz * NY + yy], depth_of(zz, y, core))

    def hop3(o, k):
        yy, zz = at_y(o), at_z(-k)
        src = a2.at[zz, yy, :, pl.ds(pl.multiple_of(24 * (1 - core), 8), 40)]
        return copy(src, a3.at[zz, yy], s3.at[zz * NY + yy], m3.at[zz * NY + yy], partner)

    load.wait()
    own = pltpu.make_async_copy(rows_of(z, y), a2.at[z, y], local_sem.at[1])
    own.start()
    for o, k in SENT[:EARLY]:
        hop1(o, k).start()
    zero = jnp.zeros((8, 128), F32)
    for p in range(2):
        fv[p, 0:8] = zero
        fv[p, 2056:2064] = zero
    def edges_of(b):
        x0 = fv[0, pl.ds(pl.multiple_of(8 + b * 128, 8), 128)]
        x1 = fv[1, pl.ds(pl.multiple_of(8 + b * 128, 8), 128)]
        both = jnp.where(lanes_of(x0.shape) < 4, pltpu.roll(x0, 2, 1), pltpu.roll(x1, 6, 1))
        return both.T[0:8]

    sub = lax.broadcasted_iota(jnp.int32, (8, 128), 0)
    lane = lanes_of((8, 128))
    is_last = sub % 4 < 2

    def pack(b, _):
        even, odd = edges_of(2 * b), edges_of(2 * b + 1)
        wlast[b] = jnp.where(is_last, even, pltpu.roll(odd, 2, 0))
        wfirst[b] = jnp.where(is_last, pltpu.roll(odd, 6, 0), even)
        return 0

    lax.fori_loop(0, 8, pack, 0)
    to_right = copy(wlast, wleft, wsend.at[0], wrecv.at[0], {"cols": right})
    to_left = copy(wfirst, wright, wsend.at[1], wrecv.at[1], {"cols": left})
    to_right.start()
    to_left.start()
    for k in TURNS[:-1]:
        hop2(0, k).start()
    own.wait()
    hop3(0, 0).start()

    def row_edges(k, _):
        yy, zz = k // NZLO, k % NZLO
        first = 8 + zz * span + yy * block
        for p in range(2):
            em[yy, zz, 4 * p:4 * p + 2] = fv[p, pl.ds(first + block, 2)]
            em[yy, zz, 4 * p + 2:4 * p + 4] = fv[p, pl.ds(first - 2, 2)]
        return 0

    lax.fori_loop(0, NY * NZLO, row_edges, 0)
    for f in range(3):
        for k in (0, 1, 130, 131):
            sf[f, k] = jnp.zeros((32, 128), F32)
    tt[0] = zero
    tt[17] = zero
    to_right.wait()
    to_left.wait()

    def join(b, _):
        wl = jnp.where(col > 0, wleft[b], 0.0)
        wr = jnp.where(col < n_cols - 1, wright[b], 0.0)
        tt[2 * b + 1] = jnp.where(is_last, wl, wr)
        tt[2 * b + 2] = jnp.where(is_last, pltpu.roll(wl, 6, 0), pltpu.roll(wr, 2, 0))
        return 0

    lax.fori_loop(0, 8, join, 0)

    def col_edges(b, _):
        before, here, after = tt[b], tt[b + 1], tt[b + 2]
        for q in range(2):
            main = pltpu.roll(here, 64, 1) if q else here
            below = pltpu.roll(after, 64, 1) if q else here
            above = pltpu.roll(here if q else before, 4 + 64 * (1 - q), 1)
            c = jnp.where(lane < 64, main, jnp.where(lane < 66, below, above))
            c = jnp.where(lane < 68, c, pltpu.roll(c, 4, 1))
            k = 2 * b + q
            em[k % NY, k // NY, 8:16] = c
        return 0

    lax.fori_loop(0, 16, col_edges, 0)

    def edge1(o, mine):
        yy = at_y(o)
        slot = y if mine else yy
        return copy(em.at[yy], e1.at[slot], es1.at[yy], er1.at[slot], depth_of(z, yy, core))

    def edge2(k, mine):
        zz = at_z(k) if mine else at_z(-k)
        slot = z if mine else zz
        return copy(e1.at[:, zz], e2.at[slot], es2.at[k], er2.at[slot], depth_of(zz, y, core))

    edge3 = copy(e2, e3, es3.at[0], er3.at[0], partner)

    for o in ORDER[1:]:
        edge1(o, True).start()
    for o, k in SENT[EARLY:]:
        hop1(o, k).start()
    e1[y] = em[y]

    def filter_xy(zz, yy, tile, edges, src_core, base):
        h = ht[zz, 64:72]
        h = jnp.where(sub < 4, pltpu.roll(h, (254 - base) % 128, 1), pltpu.roll(h, (250 - base) % 128, 1))
        g, d = along_x(edges[zz, yy, 0:8], h)
        for p in range(2):
            ug[p, 40:42] = g[4 * p:4 * p + 2]
            ug[p, 6:8] = g[4 * p + 2:4 * p + 4]
            ud[p, 40:42] = d[4 * p:4 * p + 2]
            ud[p, 6:8] = d[4 * p + 2:4 * p + 4]
        at = pl.ds(pl.multiple_of(8 - 8 * core, 8), 40)
        for p in range(2):
            h = pltpu.roll(ht[zz, pl.ds(pl.multiple_of(24 * core, 8), 40)], (254 - base - 4 * p) % 128, 1)
            g, d = along_x(tile(zz, yy, p), h)
            ug[p, at] = g
            ud[p, at] = d
        for p in range(2):
            plane = 2 + 2 * (2 * (NY * zz + yy) + src_core) + p
            a, b, c, d, e = (ug[p, 6 + k:38 + k] for k in range(5))
            sf[0, plane] = (a + e) + 4.0 * (b + d) + 6.0 * c
            sf[1, plane] = (e - a) + 2.0 * (d - b)
            a, b, c, d, e = (ud[p, 6 + k:38 + k] for k in range(5))
            sf[2, plane] = (a + e) + 4.0 * (b + d) + 6.0 * c

    def own_tile(zz, yy, p):
        return a2[zz, yy, p, pl.ds(pl.multiple_of(24 * core, 8), 40)]

    def other_tile(zz, yy, p):
        return a3[zz, yy, p]

    def render(grp):
        for j in range(4):
            s, ty, tx = ([sf[f, 4 * grp + k, 8 * j:8 * j + 8] for k in range(8)] for f in range(3))
            s, ty, tx = cascade(s), cascade(ty), cascade(tx)
            for m in range(4):
                op, w, red, green, blue = shade(s[m] + s[m + 1], s[m + 1] - s[m], ty[m] + ty[m + 1], tx[m] + tx[m + 1])
                if m == 0:
                    cr, cg, cb, ca = w * red, w * green, w * blue, op
                else:
                    rest = 1.0 - ca
                    w = rest * w
                    cr, cg, cb, ca = cr + w * red, cg + w * green, cb + w * blue, ca + rest * op
            for i, v in enumerate((cr, cg, cb, ca)):
                pim[grp, i, 8 * j:8 * j + 8] = v

    def pass_on(o, k):
        got1(o, k).wait_recv()
        (hop2 if k else hop3)(o, k).start()

    def pass_over(o, k):
        got2(o, k).wait_recv()
        hop3(o, k).start()

    def forward(o):
        for k in TURNS:
            pass_on(o, k)

    def share(o):
        for k in TURNS[:-1]:
            pass_over(o, k)

    def filter_chip(zz, yy):
        filter_xy(zz, yy, own_tile, e2, core, 8 * yy)
        filter_xy(zz, yy, other_tile, e3, 1 - core, 64 + 8 * yy)

    def step(o, low=0, high=NZLO):
        for i in range(low, high):
            hop3(o, -i).wait_recv()
        lax.fori_loop(low, high, lambda i, _: (filter_chip(at_z(i), at_y(o)), 0)[1], 0)

    def show(o, low=0, high=NZLO):
        lax.fori_loop(low, high, lambda i, _: (render((z + i) % NZLO * NY + at_y(o)), 0)[1], 0)

    forward(1)
    share(0)
    forward(-1)
    share(1)
    for o in ORDER[1:]:
        edge1(o, False).wait_recv()
    for k in range(1, NZLO):
        edge2(k, True).start()
    for i in range(NY):
        e2[z, i] = e1[i, z]
    forward(2)
    share(-1)
    for k in range(1, NZLO):
        edge2(k, False).wait_recv()
    edge3.start()
    forward(-2)
    share(2)
    share(-2)
    edge3.wait_recv()

    def turn_edges(g, _):
        tile = jnp.concatenate([e2[g, :, 8:16].reshape(64, 128), e3[g, :, 8:16].reshape(64, 128)], 0)
        ht[g] = tile.T[0:72]
        return 0

    lax.fori_loop(0, NZLO, turn_edges, 0)

    first, second, third, last = TURNS
    ticks = [(act, o, k) for act, k in ((pass_on, first), (pass_on, second), (pass_over, first), (pass_on, third),
                                        (pass_over, second), (pass_on, last), (pass_over, third)) for o in (3, -3)]
    work = [(act, o, i) for act, o in ((step, 0), (step, 1), (step, -1), (show, 0), (step, 2), (step, -2), (show, 1),
                                       (show, -1)) for i in (0, 2)]
    for n, (act, o, i) in enumerate(work):
        act(o, i, i + 2)
        if n >= 2:
            pass_piece, oo, k = ticks[n - 2]
            pass_piece(oo, k)
    for o in ORDER[1:5]:
        edge1(o, True).wait_send()
        for k in TURNS:
            hop1(o, k).wait_send()
    for o in ORDER[:5]:
        for k in TURNS[:-1]:
            hop2(o, k).wait_send()
        for k in TURNS:
            hop3(o, k).wait_send()
    for k in range(1, NZLO):
        edge2(k, True).wait_send()
    edge3.wait_send()

    def finish(k):
        hop3(4, k).wait_recv()
        zz, yy = at_z(-k), at_y(4)
        filter_chip(zz, yy)
        groups = NY * NZLO
        lax.fori_loop(0, 3, lambda i, _: (render((zz * NY + yy + i - 1 + groups) % groups), 0)[1], 0)

    step(3, 0, 2)
    pass_on(4, first)
    step(3, 2, 4)
    show(2, 0, 2)
    pass_on(4, second)
    show(2, 2, 4)
    pass_over(4, first)
    step(-3, 0, 2)
    pass_on(4, third)
    step(-3, 2, 4)
    pass_over(4, second)
    show(-2)
    finish(first)
    pass_on(4, 0)
    pass_over(4, third)
    finish(second)
    finish(0)
    finish(third)

    def over(k, acc):
        cr, cg, cb, ca = acc
        rest = 1.0 - ca
        return (cr + rest * pim[k, 0], cg + rest * pim[k, 1], cb + rest * pim[k, 2], ca + rest * pim[k, 3])

    blank = jnp.zeros((32, 128), F32)
    for i, v in enumerate(lax.fori_loop(0, n_depth // 2, over, (blank, blank, blank, blank))):
        out[i] = v

    for o in ORDER[5:]:
        edge1(o, True).wait_send()
        for k in TURNS:
            hop1(o, k).wait_send()
        for k in TURNS[:-1]:
            hop2(o, k).wait_send()
        for k in TURNS:
            hop3(o, k).wait_send()


def solution(mesh):
    n_depth, n_cols = mesh.shape["depth"], mesh.shape["cols"]

    def local(field):
        planes, total, width = field.shape
        rows = total // n_depth
        vmem = lambda *shape: pltpu.VMEM(shape, F32)
        dma = lambda n: pltpu.SemaphoreType.DMA((n,))
        return pl.pallas_call(
            functools.partial(kernel, n_depth, n_cols),
            out_shape=jax.ShapeDtypeStruct((4, rows, width), F32),
            in_specs=[pl.BlockSpec(memory_space=pltpu.HBM)],
            out_specs=pl.BlockSpec(memory_space=pltpu.VMEM),
            scratch_shapes=[
                vmem(2, total + 16, width),
                vmem(8, 8, 128), vmem(8, 8, 128), vmem(8, 8, 128), vmem(8, 8, 128), vmem(18, 8, 128),
                vmem(NY, NZLO, 16, 128), vmem(NY, NZLO, 16, 128), vmem(NZLO, NY, 16, 128), vmem(NZLO, NY, 16, 128),
                vmem(NY, NZLO - 1, 2, 64, 128), vmem(NZLO, NY, 2, 64, 128), vmem(NZLO, NY, 2, 40, 128),
                vmem(NZLO, 72, 128),
                vmem(2, 48, 128), vmem(2, 48, 128),
                vmem(3, 132, rows, width),
                vmem(n_depth // 2, 4, rows, width),
                dma(2), dma(2), dma(2),
                dma(32), dma(32), dma(32), dma(32), dma(32), dma(32),
                dma(NY), dma(NY), dma(NZLO), dma(NZLO), dma(1), dma(1),
            ],
            compiler_params=pltpu.CompilerParams(collective_id=0, has_side_effects=True, vmem_limit_bytes=63 << 20),
        )(field)

    return jax.shard_map(local, mesh=mesh, in_specs=(P("depth", None, "cols"),), out_specs=P(None, "depth", "cols"), check_vma=False)
```

```python
import functools
import math

import jax
import jax.numpy as jnp
from jax import lax
from jax.experimental import pallas as pl
from jax.experimental.pallas import tpu as pltpu
from jax.sharding import PartitionSpec as P

MESH = pl.DeviceIdType.MESH
F32 = jnp.float32
HALF = math.sqrt(0.48 * 0.48 + 0.6 * 0.6 + 1.64 * 1.64)
ORDER = (0, 1, -1, 2, -2, 3, -3, 4)
NY, NZLO = 8, 4
TURNS = (2, 3, 1, 0)
SENT = [(o, k) for d in (1, 2, 3) for k in TURNS for o in (d, -d)] + [(4, k) for k in TURNS]
EARLY = 12


def lanes_of(shape):
    return lax.broadcasted_iota(jnp.int32, shape, 1)


def along_x(x, h):
    lane = lanes_of(x.shape)
    r1 = pltpu.roll(jnp.where(lane == 127, h, x), 1, 1)
    r2 = pltpu.roll(jnp.where(lane >= 126, h, x), 2, 1)
    l1 = pltpu.roll(jnp.where(lane == 0, h, x), 127, 1)
    l2 = pltpu.roll(jnp.where(lane <= 1, h, x), 126, 1)
    gauss = (r2 + l2) + 4.0 * (r1 + l1) + 6.0 * x
    deriv = (l2 - r2) + 2.0 * (l1 - r1)
    return gauss, deriv


def cascade(v):
    for _ in range(3):
        v = [v[k] + v[k + 1] for k in range(len(v) - 1)]
    return v


def shade(s, gz, gy, gx):
    t2 = s * (14.0 / 4096.0)
    e = jnp.exp(-t2)
    sig = 1.0 / (1.0 + e)
    red = 1.0 / (1.0 + math.exp(-0.5) * e)
    op = 0.6 / (1.0 + jnp.exp(jnp.minimum(13.2 - 3.0 * t2, 87.0)))
    inv = lax.rsqrt(gx * gx + gy * gy + (gz * gz + 65536.0))
    dl = 0.48 * gx + 0.6 * gy + 0.64 * gz
    diff = jnp.maximum(dl * inv, 0.0)
    spec = jnp.maximum((dl + gz) * (inv * (1.0 / HALF)), 0.0)
    spec = spec * spec
    spec = spec * spec
    spec = spec * spec
    w = op * (0.25 + 0.6 * diff + 0.35 * spec)
    return op, w, red, 0.1 + 0.8 * sig, e * sig


def kernel(n_depth, n_cols, field, out, fv, wlast, wfirst, wleft, wright, tt, em, e1, e2, e3, a1, a2, a3, ht, ug, ud, sf, pim,
           local_sem, wsend, wrecv, s1, m1, s2, m2, s3, m3, es1, er1, es2, er2, es3, er3):
    me = lax.axis_index("depth")
    col = lax.axis_index("cols")
    z, y, core = me // (2 * NY), me // 2 % NY, me % 2
    left, right = (col + n_cols - 1) % n_cols, (col + 1) % n_cols
    block, span = 64, NY * 64

    load = pltpu.make_async_copy(field, fv.at[:, pl.ds(8, NZLO * span)], local_sem.at[0])
    load.start()

    def depth_of(zz, yy, cc):
        return {"depth": zz * (2 * NY) + yy * 2 + cc}

    def copy(src, dst, send, recv, where):
        return pltpu.make_async_remote_copy(
            src_ref=src, dst_ref=dst, send_sem=send, recv_sem=recv, device_id=where, device_id_type=MESH)

    def at_y(o):
        return (y + o + NY) % NY

    def at_z(k):
        return (z + k + NZLO) % NZLO

    partner = depth_of(z, y, 1 - core)
    barrier = pltpu.get_barrier_semaphore()

    def greet(where):
        pl.semaphore_signal(barrier, inc=1, device_id=where, device_id_type=MESH)

    for o in ORDER[1:]:
        greet(depth_of(z, at_y(o), core))
    for k in range(1, NZLO):
        greet(depth_of(at_z(k), y, core))
    greet(partner)
    greet({"cols": left})
    greet({"cols": right})
    pl.semaphore_wait(barrier, NY - 1 + NZLO - 1 + 3)

    def rows_of(zz, yy):
        return fv.at[:, pl.ds(pl.multiple_of(8 + zz * span + yy * block, 8), block)]

    def hop1(o, k):
        yy = at_y(o)
        dst = a2.at[z, y] if k == 0 else a1.at[y, k - 1]
        return copy(rows_of(at_z(k), yy), dst, s1.at[yy * NZLO + k], m1.at[y * NZLO + k], depth_of(z, yy, core))

    def got1(o, k):
        yy = at_y(o)
        dst = a2.at[z, yy] if k == 0 else a1.at[yy, k - 1]
        return copy(rows_of(at_z(k), yy), dst, s1.at[yy * NZLO + k], m1.at[yy * NZLO + k], depth_of(z, yy, core))

    def hop2(o, k):
        yy, zz = at_y(o), at_z(k)
        src = rows_of(zz, yy) if o == 0 else a1.at[yy, k - 1]
        return copy(src, a2.at[z, yy], s2.at[yy * NZLO + k], m2.at[z * NY + yy], depth_of(zz, y, core))

    def got2(o, k):
        yy, zz = at_y(o), at_z(-k)
        return copy(a2.at[zz, yy], a2.at[zz, yy], s2.at[yy * NZLO + k], m2.at[zz * NY + yy], depth_of(zz, y, core))

    def hop3(o, k):
        yy, zz = at_y(o), at_z(-k)
        src = a2.at[zz, yy, :, pl.ds(pl.multiple_of(24 * (1 - core), 8), 40)]
        return copy(src, a3.at[zz, yy], s3.at[zz * NY + yy], m3.at[zz * NY + yy], partner)

    load.wait()
    own = pltpu.make_async_copy(rows_of(z, y), a2.at[z, y], local_sem.at[1])
    own.start()
    for o, k in SENT[:EARLY]:
        hop1(o, k).start()
    zero = jnp.zeros((8, 128), F32)
    for p in range(2):
        fv[p, 0:8] = zero
        fv[p, 2056:2064] = zero
    def edges_of(b):
        x0 = fv[0, pl.ds(pl.multiple_of(8 + b * 128, 8), 128)]
        x1 = fv[1, pl.ds(pl.multiple_of(8 + b * 128, 8), 128)]
        both = jnp.where(lanes_of(x0.shape) < 4, pltpu.roll(x0, 2, 1), pltpu.roll(x1, 6, 1))
        return both.T[0:8]

    sub = lax.broadcasted_iota(jnp.int32, (8, 128), 0)
    lane = lanes_of((8, 128))
    is_last = sub % 4 < 2

    def pack(b, _):
        even, odd = edges_of(2 * b), edges_of(2 * b + 1)
        wlast[b] = jnp.where(is_last, even, pltpu.roll(odd, 2, 0))
        wfirst[b] = jnp.where(is_last, pltpu.roll(odd, 6, 0), even)
        return 0

    lax.fori_loop(0, 8, pack, 0)
    to_right = copy(wlast, wleft, wsend.at[0], wrecv.at[0], {"cols": right})
    to_left = copy(wfirst, wright, wsend.at[1], wrecv.at[1], {"cols": left})
    to_right.start()
    to_left.start()
    for k in TURNS[:-1]:
        hop2(0, k).start()
    own.wait()
    hop3(0, 0).start()

    def row_edges(k, _):
        yy, zz = k // NZLO, k % NZLO
        first = 8 + zz * span + yy * block
        for p in range(2):
            em[yy, zz, 4 * p:4 * p + 2] = fv[p, pl.ds(first + block, 2)]
            em[yy, zz, 4 * p + 2:4 * p + 4] = fv[p, pl.ds(first - 2, 2)]
        return 0

    lax.fori_loop(0, NY * NZLO, row_edges, 0)
    for f in range(3):
        for k in (0, 1, 130, 131):
            sf[f, k] = jnp.zeros((32, 128), F32)
    tt[0] = zero
    tt[17] = zero
    to_right.wait()
    to_left.wait()

    def join(b, _):
        wl = jnp.where(col > 0, wleft[b], 0.0)
        wr = jnp.where(col < n_cols - 1, wright[b], 0.0)
        tt[2 * b + 1] = jnp.where(is_last, wl, wr)
        tt[2 * b + 2] = jnp.where(is_last, pltpu.roll(wl, 6, 0), pltpu.roll(wr, 2, 0))
        return 0

    lax.fori_loop(0, 8, join, 0)

    def col_edges(b, _):
        before, here, after = tt[b], tt[b + 1], tt[b + 2]
        for q in range(2):
            main = pltpu.roll(here, 64, 1) if q else here
            below = pltpu.roll(after, 64, 1) if q else here
            above = pltpu.roll(here if q else before, 4 + 64 * (1 - q), 1)
            c = jnp.where(lane < 64, main, jnp.where(lane < 66, below, above))
            c = jnp.where(lane < 68, c, pltpu.roll(c, 4, 1))
            k = 2 * b + q
            em[k % NY, k // NY, 8:16] = c
        return 0

    lax.fori_loop(0, 16, col_edges, 0)

    def edge1(o, mine):
        yy = at_y(o)
        slot = y if mine else yy
        return copy(em.at[yy], e1.at[slot], es1.at[yy], er1.at[slot], depth_of(z, yy, core))

    def edge2(k, mine):
        zz = at_z(k) if mine else at_z(-k)
        slot = z if mine else zz
        return copy(e1.at[:, zz], e2.at[slot], es2.at[k], er2.at[slot], depth_of(zz, y, core))

    edge3 = copy(e2, e3, es3.at[0], er3.at[0], partner)

    for o in ORDER[1:]:
        edge1(o, True).start()
    for o, k in SENT[EARLY:]:
        hop1(o, k).start()
    e1[y] = em[y]

    def filter_xy(zz, yy, tile, edges, src_core, base):
        h = ht[zz, 64:72]
        h = jnp.where(sub < 4, pltpu.roll(h, (254 - base) % 128, 1), pltpu.roll(h, (250 - base) % 128, 1))
        g, d = along_x(edges[zz, yy, 0:8], h)
        for p in range(2):
            ug[p, 40:42] = g[4 * p:4 * p + 2]
            ug[p, 6:8] = g[4 * p + 2:4 * p + 4]
            ud[p, 40:42] = d[4 * p:4 * p + 2]
            ud[p, 6:8] = d[4 * p + 2:4 * p + 4]
        at = pl.ds(pl.multiple_of(8 - 8 * core, 8), 40)
        for p in range(2):
            h = pltpu.roll(ht[zz, pl.ds(pl.multiple_of(24 * core, 8), 40)], (254 - base - 4 * p) % 128, 1)
            g, d = along_x(tile(zz, yy, p), h)
            ug[p, at] = g
            ud[p, at] = d
        for p in range(2):
            plane = 2 + 2 * (2 * (NY * zz + yy) + src_core) + p
            a, b, c, d, e = (ug[p, 6 + k:38 + k] for k in range(5))
            sf[0, plane] = (a + e) + 4.0 * (b + d) + 6.0 * c
            sf[1, plane] = (e - a) + 2.0 * (d - b)
            a, b, c, d, e = (ud[p, 6 + k:38 + k] for k in range(5))
            sf[2, plane] = (a + e) + 4.0 * (b + d) + 6.0 * c

    def own_tile(zz, yy, p):
        return a2[zz, yy, p, pl.ds(pl.multiple_of(24 * core, 8), 40)]

    def other_tile(zz, yy, p):
        return a3[zz, yy, p]

    def render(grp):
        for j in range(4):
            s, ty, tx = ([sf[f, 4 * grp + k, 8 * j:8 * j + 8] for k in range(8)] for f in range(3))
            s, ty, tx = cascade(s), cascade(ty), cascade(tx)
            for m in range(4):
                op, w, red, green, blue = shade(s[m] + s[m + 1], s[m + 1] - s[m], ty[m] + ty[m + 1], tx[m] + tx[m + 1])
                if m == 0:
                    cr, cg, cb, ca = w * red, w * green, w * blue, op
                else:
                    rest = 1.0 - ca
                    w = rest * w
                    cr, cg, cb, ca = cr + w * red, cg + w * green, cb + w * blue, ca + rest * op
            for i, v in enumerate((cr, cg, cb, ca)):
                pim[grp, i, 8 * j:8 * j + 8] = v

    def pass_on(o, k):
        got1(o, k).wait_recv()
        (hop2 if k else hop3)(o, k).start()

    def pass_over(o, k):
        got2(o, k).wait_recv()
        hop3(o, k).start()

    def forward(o):
        for k in TURNS:
            pass_on(o, k)

    def share(o):
        for k in TURNS[:-1]:
            pass_over(o, k)

    def filter_chip(zz, yy):
        filter_xy(zz, yy, own_tile, e2, core, 8 * yy)
        filter_xy(zz, yy, other_tile, e3, 1 - core, 64 + 8 * yy)

    def step(o, low=0, high=NZLO):
        for i in range(low, high):
            hop3(o, -i).wait_recv()
        lax.fori_loop(low, high, lambda i, _: (filter_chip(at_z(i), at_y(o)), 0)[1], 0)

    def show(o, low=0, high=NZLO):
        lax.fori_loop(low, high, lambda i, _: (render((z + i) % NZLO * NY + at_y(o)), 0)[1], 0)

    forward(1)
    share(0)
    forward(-1)
    share(1)
    for o in ORDER[1:]:
        edge1(o, False).wait_recv()
    for k in range(1, NZLO):
        edge2(k, True).start()
    for i in range(NY):
        e2[z, i] = e1[i, z]
    forward(2)
    share(-1)
    for k in range(1, NZLO):
        edge2(k, False).wait_recv()
    edge3.start()
    forward(-2)
    share(2)
    share(-2)
    for o in (1, -1):
        edge1(o, True).wait_send()
        for k in TURNS:
            hop1(o, k).wait_send()
    for o in (0, 1, -1):
        for k in TURNS[:-1]:
            hop2(o, k).wait_send()
    for k in TURNS:
        hop3(0, k).wait_send()
    edge3.wait_recv()

    def turn_edges(g, _):
        tile = jnp.concatenate([e2[g, :, 8:16].reshape(64, 128), e3[g, :, 8:16].reshape(64, 128)], 0)
        ht[g] = tile.T[0:72]
        return 0

    lax.fori_loop(0, NZLO, turn_edges, 0)

    first, second, third, last = TURNS
    ticks = [(act, o, k) for act, k in ((pass_on, first), (pass_on, second), (pass_over, first), (pass_on, third),
                                        (pass_over, second), (pass_on, last), (pass_over, third)) for o in (3, -3)]
    work = [(act, o, i) for act, o in ((step, 0), (step, 1), (step, -1), (show, 0), (step, 2), (step, -2), (show, 1),
                                       (show, -1)) for i in (0, 2)]
    for n, (act, o, i) in enumerate(work):
        act(o, i, i + 2)
        if n >= 2:
            pass_piece, oo, k = ticks[n - 2]
            pass_piece(oo, k)
    def finish(k):
        hop3(4, k).wait_recv()
        zz, yy = at_z(-k), at_y(4)
        filter_chip(zz, yy)
        groups = NY * NZLO
        lax.fori_loop(0, 3, lambda i, _: (render((zz * NY + yy + i - 1 + groups) % groups), 0)[1], 0)

    step(3, 0, 2)
    pass_on(4, first)
    step(3, 2, 4)
    show(2, 0, 2)
    pass_on(4, second)
    show(2, 2, 4)
    pass_over(4, first)
    step(-3, 0, 2)
    pass_on(4, third)
    step(-3, 2, 4)
    pass_over(4, second)
    show(-2)
    finish(first)
    for o in (2, -2):
        edge1(o, True).wait_send()
        for k in TURNS:
            hop1(o, k).wait_send()
        for k in TURNS[:-1]:
            hop2(o, k).wait_send()
    for k in range(1, NZLO):
        edge2(k, True).wait_send()
    edge3.wait_send()
    for o in ORDER[1:5]:
        for k in TURNS:
            hop3(o, k).wait_send()
    pass_on(4, 0)
    pass_over(4, third)
    finish(second)
    finish(0)
    finish(third)

    def over(k, acc):
        cr, cg, cb, ca = acc
        rest = 1.0 - ca
        return (cr + rest * pim[k, 0], cg + rest * pim[k, 1], cb + rest * pim[k, 2], ca + rest * pim[k, 3])

    blank = jnp.zeros((32, 128), F32)
    for i, v in enumerate(lax.fori_loop(0, n_depth // 2, over, (blank, blank, blank, blank))):
        out[i] = v

    for o in ORDER[5:]:
        edge1(o, True).wait_send()
        for k in TURNS:
            hop1(o, k).wait_send()
        for k in TURNS[:-1]:
            hop2(o, k).wait_send()
        for k in TURNS:
            hop3(o, k).wait_send()


def solution(mesh):
    n_depth, n_cols = mesh.shape["depth"], mesh.shape["cols"]

    def local(field):
        planes, total, width = field.shape
        rows = total // n_depth
        vmem = lambda *shape: pltpu.VMEM(shape, F32)
        dma = lambda n: pltpu.SemaphoreType.DMA((n,))
        return pl.pallas_call(
            functools.partial(kernel, n_depth, n_cols),
            out_shape=jax.ShapeDtypeStruct((4, rows, width), F32),
            in_specs=[pl.BlockSpec(memory_space=pltpu.HBM)],
            out_specs=pl.BlockSpec(memory_space=pltpu.VMEM),
            scratch_shapes=[
                vmem(2, total + 16, width),
                vmem(8, 8, 128), vmem(8, 8, 128), vmem(8, 8, 128), vmem(8, 8, 128), vmem(18, 8, 128),
                vmem(NY, NZLO, 16, 128), vmem(NY, NZLO, 16, 128), vmem(NZLO, NY, 16, 128), vmem(NZLO, NY, 16, 128),
                vmem(NY, NZLO - 1, 2, 64, 128), vmem(NZLO, NY, 2, 64, 128), vmem(NZLO, NY, 2, 40, 128),
                vmem(NZLO, 72, 128),
                vmem(2, 48, 128), vmem(2, 48, 128),
                vmem(3, 132, rows, width),
                vmem(n_depth // 2, 4, rows, width),
                dma(2), dma(2), dma(2),
                dma(32), dma(32), dma(32), dma(32), dma(32), dma(32),
                dma(NY), dma(NY), dma(NZLO), dma(NZLO), dma(1), dma(1),
            ],
            compiler_params=pltpu.CompilerParams(collective_id=0, has_side_effects=True, vmem_limit_bytes=63 << 20),
        )(field)

    return jax.shard_map(local, mesh=mesh, in_specs=(P("depth", None, "cols"),), out_specs=P(None, "depth", "cols"), check_vma=False)
```
